1024 devices in a mesh: outer: 64 (over z, y_lo, core), inner: 16 (over y_hi, x).
Axes of the slice: x: 4, y: 8 (y_hi: 4, y_lo: 2; y = y_hi * 2 + y_lo), z: 16, core: 2. Of those that a mesh axis runs over, the one named last changes fastest.
Arguments:
- tokens: bfloat16 [131072, 12288], P(('outer', 'inner')), may hold values from -16 to 16
- cotangent: bfloat16 [131072, 128], P(('outer', 'inner')), may hold values from -8 to 8
- secondary: bfloat16 [12288, 128], P('inner'), may hold values from -0.0546875 to 0.0546875
- master: float32 [12288, 128], P(('inner', 'outer')), may hold values from -6 to 6
- m_code: bfloat16 [12288, 128], P(('inner', 'outer')), may hold values from -1 to 1
- v_code: bfloat16 [12288, 128], P(('inner', 'outer')), may hold values from 0.049804688 to 1
- m_scale: float32 [3072], P(('inner', 'outer')), may hold values from 0.02 to 0.2
- v_scale: float32 [3072], P(('inner', 'outer')), may hold values from 0.001 to 0.02
Outputs:
- projected: bfloat16 [131072, 128], P(('outer', 'inner'))
- master_new: float32 [12288, 128], P(('inner', 'outer'))
- m_code_new: bfloat16 [12288, 128], P(('inner', 'outer'))
- v_code_new: bfloat16 [12288, 128], P(('inner', 'outer'))
- m_scale_new: float32 [3072], P(('inner', 'outer'))
- v_scale_new: float32 [3072], P(('inner', 'outer'))
- secondary_new: bfloat16 [12288, 128], P('inner')
The draws below stay inside these ranges and needn't reach their ends.
All inputs are finite; a program needn't handle non-finite values. Where the reference program divides by a largest or mean magnitude, that divisor is 1e-20 or more.
Results may differ from the reference program's by a relative error of at most 0.009.
Values may be sent and summed in bfloat16 or wider, within the bound.
No kernel may reach another device: no remote copies, remote signals or barrier semaphores. Data moves between devices by JAX's collectives and lax.ppermute only.
A program may use at most 32 MiB of HBM per device.

```python
import math
import jax
import jax.numpy as jnp
from jax import lax

D = 12288
HEAD = 128
TOK_DEV = 128
TOKENS = 131072
BLOCKS = 3072
N_OUTER = 64
N_INNER = 16


def shared_signs(key):
    drawn = jax.random.randint(jax.random.fold_in(key, 31), (TOKENS,), 0, 2)
    return drawn.astype(jnp.float32) * 2.0 - 1.0


def shared_weight():
    return 2.0 ** 0.5 / float(TOKENS) ** 0.25


def draw_tokens(key, part):
    devices = TOKENS // TOK_DEV
    shard_rows = D // devices
    column = jnp.arange(D, dtype=jnp.int32)
    owner = column // shard_rows
    outer_index = (owner % N_OUTER).astype(jnp.float32)
    variance = 0.5 + outer_index / max(N_OUTER - 1, 1)
    amplitude = jnp.sqrt(variance)
    base = jax.random.normal(jax.random.fold_in(key, 11), (TOKENS, D), jnp.float32)
    base = jnp.clip(base, -4.0, 4.0)
    pairing = jax.random.permutation(jax.random.fold_in(key, 12), devices).astype(jnp.int32)
    row_group = jnp.arange(TOKENS, dtype=jnp.int32) // TOK_DEV
    spiked = pairing[row_group][:, None] == owner[None, :]
    boost = jnp.where(spiked, 6.0, 1.0)
    direction = jnp.clip(jax.random.normal(jax.random.fold_in(key, 13), (D,), jnp.float32), -3.0, 3.0)
    signs = shared_signs(key)
    common = shared_weight() * signs[:, None] * direction[None, :]
    values = (base * boost + common) * amplitude[None, :]
    return jnp.clip(values, -16.0, 16.0).astype(jnp.bfloat16)


def draw_cotangent(key, part):
    base = jnp.clip(jax.random.normal(jax.random.fold_in(key, 41), (TOKENS, HEAD), jnp.float32), -4.0, 4.0)
    direction = jnp.clip(jax.random.normal(jax.random.fold_in(key, 42), (HEAD,), jnp.float32), -3.0, 3.0)
    signs = shared_signs(key)
    values = base + shared_weight() * signs[:, None] * direction[None, :]
    return jnp.clip(values, -8.0, 8.0).astype(jnp.bfloat16)


def levels(key, dims, split, low, high):
    factor_of, own = 1.0, jax.random.fold_in(key, 6)
    for position, shards_of in split:
        heights = jnp.exp(jax.random.uniform(jax.random.fold_in(own, position), (shards_of,), jnp.float32, low / len(split), high / len(split)))
        factor_of = factor_of * jnp.repeat(heights, dims[position] // shards_of).reshape([-1 if axis == position else 1 for axis in range(len(dims))])
    return factor_of


def gaussian(stream_key, extent, deviation, bound, pieces=(), held_as=jnp.bfloat16):
    loudness = levels(stream_key, extent, pieces, -0.22, 0.18) if pieces else 1.0
    array = jax.random.normal(stream_key, extent, jnp.float32) * deviation * loudness
    return jnp.minimum(jnp.maximum(array, -bound), bound).astype(held_as)


def setup_inputs(seed: int = 0) -> dict:
    splits = jax.random.split(jax.random.key(seed), 9)
    return {
        "tokens": draw_tokens(jax.random.fold_in(splits[8], 71), 0),
        "cotangent": draw_cotangent(jax.random.fold_in(splits[8], 71), 0),
        "secondary": gaussian(splits[2], (D, HEAD), D ** -0.5, 0.0546875, ((0, 16),)),
        "master": gaussian(splits[3], (D, HEAD), 1.0, 6.0, ((0, 1024),), jnp.float32),
        "m_code": jnp.clip(jax.random.uniform(splits[4], (D, HEAD), jnp.float32, -1.0, 1.0) * levels(splits[4], (D, HEAD), ((0, 1024),), -0.4, 0.0), -1.0, 1.0).astype(jnp.bfloat16),
        "v_code": jnp.clip(0.049804688 + 0.9501953 * jax.random.uniform(splits[5], (D, HEAD), jnp.float32) ** levels(splits[5], (D, HEAD), ((0, 1024),), -0.2, 0.2), 0.049804688, 1.0).astype(jnp.bfloat16),
        "m_scale": jnp.clip(jnp.exp(math.log(0.2) - 2.3025851 * jax.random.uniform(splits[6], (BLOCKS,), jnp.float32) ** levels(splits[6], (BLOCKS,), ((0, 1024),), -0.2, 0.2)), 0.02, 0.2),
        "v_scale": jnp.clip(jnp.exp(math.log(0.02) - 2.9957322 * jax.random.uniform(splits[7], (BLOCKS,), jnp.float32) ** levels(splits[7], (BLOCKS,), ((0, 1024),), -0.2, 0.2)), 0.001, 0.02),
    }


def adam_update(gradient, factor, master, m_code, v_code, m_scale, v_scale):
    blocks = m_scale.shape[0]
    height = master.shape[0] // blocks
    shaped = (blocks, height, master.shape[1])
    m_old = (m_code.astype(jnp.float32).reshape(shaped) * m_scale[:, None, None]).reshape(master.shape)
    v_old = (v_code.astype(jnp.float32).reshape(shaped) * v_scale[:, None, None]).reshape(master.shape)
    scaled = factor * gradient
    moment = 0.9 * m_old + 0.1 * scaled
    second = 0.95 * v_old + 0.05 * scaled * scaled
    master_new = master - 0.01 * (moment / (jnp.sqrt(second) + 1e-08) + 0.1 * master)
    moment_blocks = moment.reshape(blocks, -1)
    second_blocks = second.reshape(blocks, -1)
    m_scale_new = lax.optimization_barrier(jnp.max(jnp.abs(moment_blocks), axis=1)) + 1e-06
    v_scale_new = lax.optimization_barrier(jnp.max(second_blocks, axis=1)) + 1e-06
    m_code_new = (moment_blocks / m_scale_new[:, None]).reshape(master.shape).astype(jnp.bfloat16)
    v_code_new = (second_blocks / v_scale_new[:, None]).reshape(master.shape).astype(jnp.bfloat16)
    return (master_new, m_code_new, v_code_new, m_scale_new, v_scale_new)

def reference(tokens, cotangent, secondary, master, m_code, v_code, m_scale, v_scale):
    projected = jnp.dot(tokens, secondary, preferred_element_type=jnp.float32).astype(jnp.bfloat16)
    groups = N_OUTER * N_INNER
    tok_blocks = tokens.reshape(groups, TOK_DEV, D)
    cot_blocks = cotangent.reshape(groups, TOK_DEV, HEAD)

    def accumulate(total, pair):
        part = lax.dot_general(pair[0], pair[1], (((0,), (0,)), ((), ())), preferred_element_type=jnp.float32)
        part = lax.optimization_barrier(part.astype(jnp.bfloat16))
        return (total + part.astype(jnp.float32), None)
    gradient, _ = lax.scan(accumulate, jnp.zeros((D, HEAD), jnp.float32), (tok_blocks, cot_blocks))
    total = jnp.sum(gradient * gradient)
    limit = 0.25 * math.sqrt(D * HEAD)
    factor = limit / jnp.maximum(jnp.sqrt(total), limit)
    master_new, m_code_new, v_code_new, m_scale_new, v_scale_new = adam_update(gradient, factor, master, m_code, v_code, m_scale, v_scale)
    secondary_new = master_new.astype(jnp.bfloat16)
    return (projected, master_new, m_code_new, v_code_new, m_scale_new, v_scale_new, secondary_new)
```

```python
import math

import jax
import jax.numpy as jnp
from jax import lax
from jax.sharding import Mesh
from jax.sharding import PartitionSpec as P

INNER = ("yh", "x")
OUTER = ("z", "yl", "c")
OUTER_INNER = OUTER + INNER
INNER_OUTER = INNER + OUTER
bf16, f32 = jnp.bfloat16, jnp.float32


def exchange(pieces, axes):
    return lax.all_to_all(pieces, axes, split_axis=0, concat_axis=0, tiled=True)


def to_all(value, axes):
    return exchange(jnp.broadcast_to(value, (lax.axis_size(axes), *value.shape)), axes)


def adam_update(gradient, factor, master, m_code, v_code, m_scale, v_scale):
    blocks = m_scale.shape[0]
    height = master.shape[0] // blocks
    shaped = (blocks, height, master.shape[1])
    m_old = (m_code.astype(f32).reshape(shaped) * m_scale[:, None, None]).reshape(master.shape)
    v_old = (v_code.astype(f32).reshape(shaped) * v_scale[:, None, None]).reshape(master.shape)
    scaled = factor * gradient
    moment = 0.9 * m_old + 0.1 * scaled
    second = 0.95 * v_old + 0.05 * scaled * scaled
    master_new = master - 0.01 * (moment / (jnp.sqrt(second) + 1e-08) + 0.1 * master)
    moment_blocks = moment.reshape(blocks, -1)
    second_blocks = second.reshape(blocks, -1)
    m_scale_new = jnp.max(jnp.abs(moment_blocks), axis=1) + 1e-06
    v_scale_new = jnp.max(second_blocks, axis=1) + 1e-06
    m_code_new = (moment_blocks / m_scale_new[:, None]).reshape(master.shape).astype(bf16)
    v_code_new = (second_blocks / v_scale_new[:, None]).reshape(master.shape).astype(bf16)
    return (master_new, m_code_new, v_code_new, m_scale_new, v_scale_new)


def body(tokens, cotangent, secondary, master, m_code, v_code, m_scale, v_scale):
    width, head = tokens.shape[1], cotangent.shape[1]
    rows = master.shape[0]
    gathered = lax.all_gather(secondary, INNER, axis=0, tiled=True)
    part = lax.dot_general(
        tokens, cotangent, (((0,), (0,)), ((), ())), preferred_element_type=f32
    )
    nyh, nx, nz, nyl = (lax.axis_size(a) for a in ("yh", "x", "z", "yl"))
    part = part.reshape(nyh, nx, nz, nyl, 2, rows, head)
    part = part.transpose(4, 1, 3, 0, 2, 5, 6).reshape(2, nx * nyl, nyh * nz * rows, head)
    part = lax.optimization_barrier(part.astype(bf16))
    mine = lax.axis_index("c") == 0
    kept = jnp.where(mine, part[0], part[1])
    sent = jnp.where(mine, part[1], part[0])
    other = lax.ppermute(sent, "c", [(0, 1), (1, 0)])
    group = (kept.astype(f32) + other.astype(f32)).astype(bf16)
    group = jnp.sum(exchange(group, ("x", "yl")).astype(f32), axis=0).astype(bf16)
    group = exchange(group.reshape(nyh, nz * rows, head), "yh")
    group = jnp.sum(group.astype(f32), axis=0).astype(bf16)
    group = exchange(group.reshape(nz, rows, head), "z")
    gradient = jnp.sum(group.astype(f32), axis=0)
    total = jnp.sum(gradient * gradient)
    total = jnp.sum(to_all(jnp.broadcast_to(total, (1, head)), INNER), axis=0)
    total = jnp.sum(to_all(total, OUTER), axis=0)[0, 0]
    limit = 0.25 * math.sqrt(width * head)
    factor = limit / jnp.maximum(jnp.sqrt(total), limit)
    master_new, m_code_new, v_code_new, m_scale_new, v_scale_new = adam_update(
        gradient, factor, master, m_code, v_code, m_scale, v_scale
    )
    secondary_new = to_all(master_new.astype(bf16), OUTER).reshape(secondary.shape)
    projected = jnp.dot(tokens, gathered, preferred_element_type=f32).astype(bf16)
    return (projected, master_new, m_code_new, v_code_new, m_scale_new, v_scale_new, secondary_new)


def solution(mesh):
    split = Mesh(mesh.devices.reshape(16, 2, 2, 4, 4), OUTER_INNER)
    return jax.shard_map(
        body,
        mesh=split,
        in_specs=(
            P(OUTER_INNER, None),
            P(OUTER_INNER, None),
            P(INNER, None),
            P(INNER_OUTER, None),
            P(INNER_OUTER, None),
            P(INNER_OUTER, None),
            P(INNER_OUTER),
            P(INNER_OUTER),
        ),
        out_specs=(
            P(OUTER_INNER, None),
            P(INNER_OUTER, None),
            P(INNER_OUTER, None),
            P(INNER_OUTER, None),
            P(INNER_OUTER),
            P(INNER_OUTER),
            P(INNER, None),
        ),
        check_vma=False,
    )
```

```python
import functools
import math

import jax
import jax.numpy as jnp
from jax import lax
from jax.experimental import pallas as pl
from jax.experimental.pallas import tpu as pltpu
from jax.sharding import Mesh
from jax.sharding import PartitionSpec as P

INNER = ("yh", "x")
OUTER = ("zh", "zl", "yl", "c")
OUTER_INNER = OUTER + INNER
INNER_OUTER = INNER + OUTER
NZ, NYL, NC, NYH, NX = 16, 2, 2, 4, 4
SLOT = 16
bf16, f32 = jnp.bfloat16, jnp.float32
WHOLE = pl.BlockSpec(memory_space=pltpu.VMEM)
SCALARS = pl.BlockSpec(memory_space=pltpu.SMEM)


def exchange(pieces, axes):
    return lax.all_to_all(pieces, axes, split_axis=0, concat_axis=0, tiled=True)


def to_all(value, axes):
    return exchange(jnp.broadcast_to(value, (lax.axis_size(axes), *value.shape)), axes)


def swap_cores(value):
    return lax.ppermute(value, "c", [(0, 1), (1, 0)])


def gradient_kernel(
    rows, core_ref, m_scale_ref, v_scale_ref, tokens_ref, cotangent_ref, master_ref, m_code_ref,
    v_code_ref, kept_ref, sent_ref, states_ref,
):
    first = core_ref[0] == 0

    @pl.when(pl.program_id(0) == 0)
    def _():
        height = rows // m_scale_ref.shape[0]
        line = lax.broadcasted_iota(jnp.int32, master_ref.shape, 0)
        m_scale, v_scale = m_scale_ref[0], v_scale_ref[0]
        for b in range(1, m_scale_ref.shape[0]):
            m_scale = jnp.where(line < b * height, m_scale, m_scale_ref[b])
            v_scale = jnp.where(line < b * height, v_scale, v_scale_ref[b])
        master = master_ref[...]
        high = master.astype(bf16).astype(f32)
        pad = jnp.ones((SLOT - rows, master.shape[1]), f32)
        slots = (
            m_code_ref[...].astype(f32) * m_scale,
            v_code_ref[...].astype(f32) * v_scale,
            high,
            master - high,
        )
        for k, slot in enumerate(slots):
            states_ref[k * SLOT : (k + 1) * SLOT, :] = jnp.concatenate([slot, pad], axis=0).astype(bf16)

    part = lax.dot_general(
        tokens_ref[...], cotangent_ref[...], (((0,), (0,)), ((), ())), preferred_element_type=f32
    )
    chip = NC * rows
    for yl in range(NYL):
        for quad in range(NZ // 4):
            both = []
            for core in range(NC):
                starts = [
                    ((4 * quad + j) * NYL + yl) * chip + core * rows for j in range(4)
                ]
                both.append(jnp.concatenate([part[s : s + rows] for s in starts], axis=0))
            at = slice(quad * 4 * rows, (quad + 1) * 4 * rows)
            kept_ref[0, yl, 0, at, :] = jnp.where(first, both[0], both[1]).astype(bf16)
            sent_ref[0, yl, 0, at, :] = jnp.where(first, both[1], both[0]).astype(bf16)


def gradient_parts(core, tokens, cotangent, master, m_code, v_code, m_scale, v_scale):
    rows = master.shape[0]
    count, width = tokens.shape
    head = cotangent.shape[1]
    columns = width // (NYH * NX)
    shape = jax.ShapeDtypeStruct((NX, NYL, NYH, NZ * rows, head), bf16)
    spec = pl.BlockSpec((1, NYL, 1, NZ * rows, head), lambda i: (i % NX, 0, i // NX, 0, 0))
    return pl.pallas_call(
        functools.partial(gradient_kernel, rows),
        grid=(NYH * NX,),
        in_specs=[
            SCALARS,
            SCALARS,
            SCALARS,
            pl.BlockSpec((count, columns), lambda i: (0, i)),
            pl.BlockSpec((count, head), lambda i: (0, 0)),
        ]
        + [pl.BlockSpec((rows, head), lambda i: (0, 0))] * 3,
        out_specs=[spec, spec, pl.BlockSpec((4 * SLOT, head), lambda i: (0, 0))],
        out_shape=[shape, shape, jax.ShapeDtypeStruct((4 * SLOT, head), bf16)],
        name="gradient_parts",
    )(core, m_scale, v_scale, tokens, cotangent, master, m_code, v_code)


def forward_kernel(core_ref, tokens_ref, mine_ref, other_ref, out_ref, total_ref):
    step = pl.program_id(0)

    @pl.when(step == 0)
    def _():
        total_ref[...] = jnp.zeros_like(total_ref)

    half = mine_ref.shape[0]
    core = core_ref[0]
    own = tokens_ref[:, pl.ds(pl.multiple_of(core * half, half), half)]
    rest = tokens_ref[:, pl.ds(pl.multiple_of((1 - core) * half, half), half)]
    total_ref[...] += jnp.dot(own, mine_ref[...], preferred_element_type=f32) + jnp.dot(
        rest, other_ref[...], preferred_element_type=f32
    )

    @pl.when(step == pl.num_programs(0) - 1)
    def _():
        out_ref[...] = total_ref[...].astype(bf16)


def forward(core, tokens, mine, other):
    count, width = tokens.shape
    head = mine.shape[1]
    shards = NYH * NX
    half = mine.shape[0] // shards
    weight = pl.BlockSpec((half, head), lambda i: (i, 0))
    return pl.pallas_call(
        forward_kernel,
        grid=(shards,),
        in_specs=[SCALARS, pl.BlockSpec((count, width // shards), lambda i: (0, i)), weight, weight],
        out_specs=pl.BlockSpec((count, head), lambda i: (0, 0)),
        out_shape=jax.ShapeDtypeStruct((count, head), bf16),
        scratch_shapes=[pltpu.VMEM((count, head), f32)],
        name="forward",
    )(core, tokens, mine, other)


def update_kernel(
    limit, place_ref, squares_ref, sums_ref, all_sums_ref, states_ref, master_ref, m_code_ref,
    v_code_ref, m_scale_ref, v_scale_ref, master_new_ref, m_code_new_ref, v_code_new_ref,
    m_scale_new_ref, v_scale_new_ref, secondary_ref,
):
    rows, head = master_ref.shape
    blocks = m_scale_ref.shape[0]
    height = rows // blocks
    total = jnp.sum(squares_ref[...], axis=0, keepdims=True)
    factor = limit / jnp.maximum(jnp.sqrt(total), limit)
    gradient = sums_ref[pl.ds(place_ref[0] * rows, rows), :]
    for b in range(blocks):
        at = slice(b * height, (b + 1) * height)
        scaled = factor * gradient[at]
        m_old = m_code_ref[...].astype(f32)[at] * m_scale_ref[b]
        v_old = v_code_ref[...].astype(f32)[at] * v_scale_ref[b]
        moment = 0.9 * m_old + 0.1 * scaled
        second = 0.95 * v_old + 0.05 * scaled * scaled
        old = master_ref[at, :]
        master_new_ref[at, :] = old - 0.01 * (moment / (jnp.sqrt(second) + 1e-08) + 0.1 * old)
        m_top = jnp.max(jnp.abs(moment)) + 1e-06
        v_top = jnp.max(second) + 1e-06
        m_scale_new_ref[b] = m_top
        v_scale_new_ref[b] = v_top
        m_code_new_ref[at, :] = (moment / m_top).astype(bf16)
        v_code_new_ref[at, :] = (second / v_top).astype(bf16)
    pad = jnp.zeros((SLOT - rows, head), f32)
    for quad in range(NZ // 4):
        span = slice(quad * 4 * rows, (quad + 1) * 4 * rows)
        sums = [all_sums_ref[k, span, :].astype(f32) for k in range(NYL * NC)]
        new = []
        for j in range(4):
            for k in range(NYL * NC):
                scaled = factor * jnp.concatenate([sums[k][j * rows : (j + 1) * rows], pad], axis=0)
                device = (4 * quad + j) * NYL * NC + k
                m_old, v_old, high, low = (
                    states_ref[device, s * SLOT : (s + 1) * SLOT, :].astype(f32) for s in range(4)
                )
                old = high + low
                moment = 0.9 * m_old + 0.1 * scaled
                second = 0.95 * v_old + 0.05 * scaled * scaled
                value = old - 0.01 * (moment / (jnp.sqrt(second) + 1e-08) + 0.1 * old)
                new.append(value[:rows])
        out = slice(quad * 4 * NYL * NC * rows, (quad + 1) * 4 * NYL * NC * rows)
        secondary_ref[out, :] = jnp.concatenate(new, axis=0).astype(bf16)


def update(limit, place, squares, sums, all_sums, states, master, m_code, v_code, m_scale, v_scale, copy_rows):
    shape = jax.ShapeDtypeStruct
    return pl.pallas_call(
        functools.partial(update_kernel, limit),
        in_specs=[SCALARS] + [WHOLE] * 7 + [SCALARS] * 2,
        out_specs=[WHOLE] * 3 + [SCALARS] * 2 + [WHOLE],
        out_shape=[
            shape(master.shape, f32),
            shape(m_code.shape, bf16),
            shape(v_code.shape, bf16),
            shape(m_scale.shape, f32),
            shape(v_scale.shape, f32),
            shape((copy_rows, master.shape[1]), bf16),
        ],
        name="update",
    )(place, squares, sums, all_sums, states, master, m_code, v_code, m_scale, v_scale)


def body(tokens, cotangent, secondary, master, m_code, v_code, m_scale, v_scale):
    width, head = tokens.shape[1], cotangent.shape[1]
    rows, copy_rows = master.shape[0], secondary.shape[0]
    core = lax.axis_index("c")
    cores = core.reshape(1).astype(jnp.int32)
    kept, sent, own_states = gradient_parts(
        cores, tokens, cotangent, master, m_code, v_code, m_scale, v_scale
    )
    states = lax.all_gather(own_states, OUTER, axis=0, tiled=False)
    kept = kept.reshape(NX * NYL, NYH * NZ * rows, head)
    other = swap_cores(sent.reshape(kept.shape))
    group = (kept.astype(f32) + other.astype(f32)).astype(bf16)
    group = exchange(group, ("x", "yl"))
    group = jnp.sum(group.astype(f32), axis=0).astype(bf16)
    weight = lax.dynamic_slice_in_dim(secondary, core * (copy_rows // 2), copy_rows // 2, 0)
    group, weight, states = lax.optimization_barrier((group, weight, states))
    mine = lax.all_gather(weight, INNER, axis=0, tiled=True)
    group = exchange(group.reshape(NYH, NZ * rows, head), "yh")
    group = jnp.sum(group.astype(f32), axis=0).astype(bf16)
    group = jnp.sum(to_all(group, "zl").astype(f32), axis=0).astype(bf16)
    sums = jnp.sum(to_all(group, "zh").astype(f32), axis=0)
    all_sums = to_all(sums.astype(bf16), ("yl", "c"))
    all_sums, mine = lax.optimization_barrier((all_sums, mine))
    squares = jnp.sum(jnp.square(all_sums.astype(f32)))
    squares = to_all(jnp.broadcast_to(squares, (1, head)), INNER).reshape(NYH * NX, head)
    projected = forward(cores, tokens, mine, swap_cores(mine))
    squares, projected = lax.optimization_barrier((squares, projected))
    limit = 0.25 * math.sqrt(width * head)
    place = (lax.axis_index("zh") * 4 + lax.axis_index("zl")).reshape(1).astype(jnp.int32)
    results = update(
        limit, place, squares, sums, all_sums, states, master, m_code, v_code, m_scale, v_scale, copy_rows
    )
    return (projected, *results)


def solution(mesh):
    split = Mesh(mesh.devices.reshape(4, 4, 2, 2, 4, 4), OUTER_INNER)
    return jax.shard_map(
        body,
        mesh=split,
        in_specs=(
            P(OUTER_INNER, None),
            P(OUTER_INNER, None),
            P(INNER, None),
            P(INNER_OUTER, None),
            P(INNER_OUTER, None),
            P(INNER_OUTER, None),
            P(INNER_OUTER),
            P(INNER_OUTER),
        ),
        out_specs=(
            P(OUTER_INNER, None),
            P(INNER_OUTER, None),
            P(INNER_OUTER, None),
            P(INNER_OUTER, None),
            P(INNER_OUTER),
            P(INNER_OUTER),
            P(INNER, None),
        ),
        check_vma=False,
    )
```

```python
import functools
import math

import jax
import jax.numpy as jnp
from jax import lax
from jax.experimental import pallas as pl
from jax.experimental.pallas import tpu as pltpu
from jax.sharding import Mesh
from jax.sharding import PartitionSpec as P

INNER = ("yh", "x")
OUTER = ("zh", "zl", "yl", "c")
OUTER_INNER = OUTER + INNER
INNER_OUTER = INNER + OUTER
NEAR = ("zl", "yl", "c")
NZH, NZL, NYL, NC, NYH, NX = 4, 4, 2, 2, 4, 4
SLOT = 16
bf16, f32 = jnp.bfloat16, jnp.float32
WHOLE = pl.BlockSpec(memory_space=pltpu.VMEM)
SCALARS = pl.BlockSpec(memory_space=pltpu.SMEM)


def exchange(pieces, axes):
    return lax.all_to_all(pieces, axes, split_axis=0, concat_axis=0, tiled=True)


def to_all(value, axes):
    return exchange(jnp.broadcast_to(value, (lax.axis_size(axes), *value.shape)), axes)


def swap_cores(value):
    return lax.ppermute(value, "c", [(0, 1), (1, 0)])


def gradient_kernel(
    rows, core_ref, m_scale_ref, v_scale_ref, tokens_ref, cotangent_ref, master_ref, m_code_ref,
    v_code_ref, kept_ref, sent_ref, states_ref,
):
    first = core_ref[0] == 0

    @pl.when(pl.program_id(0) == 0)
    def _():
        height = rows // m_scale_ref.shape[0]
        line = lax.broadcasted_iota(jnp.int32, master_ref.shape, 0)
        m_scale, v_scale = m_scale_ref[0], v_scale_ref[0]
        for b in range(1, m_scale_ref.shape[0]):
            m_scale = jnp.where(line < b * height, m_scale, m_scale_ref[b])
            v_scale = jnp.where(line < b * height, v_scale, v_scale_ref[b])
        master = master_ref[...]
        high = master.astype(bf16).astype(f32)
        pad = jnp.ones((SLOT - rows, master.shape[1]), f32)
        slots = (
            m_code_ref[...].astype(f32) * m_scale,
            v_code_ref[...].astype(f32) * v_scale,
            high,
            master - high,
        )
        for k, slot in enumerate(slots):
            states_ref[k * SLOT : (k + 1) * SLOT, :] = jnp.concatenate([slot, pad], axis=0).astype(bf16)

    columns = tokens_ref.shape[1] // NX
    chip = NC * rows
    for x in range(NX):
        part = lax.dot_general(
            tokens_ref[:, x * columns : (x + 1) * columns],
            cotangent_ref[...],
            (((0,), (0,)), ((), ())),
            preferred_element_type=f32,
        )
        for yl in range(NYL):
            for zl in range(NZL):
                both = []
                for core in range(NC):
                    starts = [
                        ((NZL * zh + zl) * NYL + yl) * chip + core * rows for zh in range(NZH)
                    ]
                    both.append(jnp.concatenate([part[s : s + rows] for s in starts], axis=0))
                at = slice(zl * NZH * rows, (zl + 1) * NZH * rows)
                kept_ref[x, yl, 0, at, :] = jnp.where(first, both[0], both[1]).astype(bf16)
                sent_ref[x, yl, 0, at, :] = jnp.where(first, both[1], both[0]).astype(bf16)


def gradient_parts(core, tokens, cotangent, master, m_code, v_code, m_scale, v_scale):
    rows = master.shape[0]
    count, width = tokens.shape
    head = cotangent.shape[1]
    span = NZH * NZL * rows
    shape = jax.ShapeDtypeStruct((NX, NYL, NYH, span, head), bf16)
    spec = pl.BlockSpec((NX, NYL, 1, span, head), lambda i: (0, 0, i, 0, 0))
    return pl.pallas_call(
        functools.partial(gradient_kernel, rows),
        grid=(NYH,),
        in_specs=[
            SCALARS,
            SCALARS,
            SCALARS,
            pl.BlockSpec((count, width // NYH), lambda i: (0, i)),
            pl.BlockSpec((count, head), lambda i: (0, 0)),
        ]
        + [pl.BlockSpec((rows, head), lambda i: (0, 0))] * 3,
        out_specs=[spec, spec, pl.BlockSpec((4 * SLOT, head), lambda i: (0, 0))],
        out_shape=[shape, shape, jax.ShapeDtypeStruct((4 * SLOT, head), bf16)],
        name="gradient_parts",
    )(core, m_scale, v_scale, tokens, cotangent, master, m_code, v_code)


def forward_kernel(core_ref, tokens_ref, mine_ref, other_ref, out_ref, total_ref):
    step = pl.program_id(0)
    core = core_ref[0]
    half = mine_ref.shape[0] // NX
    total = jnp.zeros(total_ref.shape, f32)
    for x in range(NX):
        own = pl.ds(pl.multiple_of((2 * x + core) * half, half), half)
        rest = pl.ds(pl.multiple_of((2 * x + 1 - core) * half, half), half)
        at = slice(x * half, (x + 1) * half)
        total += jnp.dot(tokens_ref[:, own], mine_ref[at, :], preferred_element_type=f32)
        total += jnp.dot(tokens_ref[:, rest], other_ref[at, :], preferred_element_type=f32)

    @pl.when(step == 0)
    def _():
        total_ref[...] = total

    @pl.when(step > 0)
    def _():
        total_ref[...] += total

    @pl.when(step == pl.num_programs(0) - 1)
    def _():
        out_ref[...] = total_ref[...].astype(bf16)


def forward(core, tokens, mine, other):
    count, width = tokens.shape
    height, head = mine.shape
    weight = pl.BlockSpec((height // NYH, head), lambda i: (i, 0))
    return pl.pallas_call(
        forward_kernel,
        grid=(NYH,),
        in_specs=[SCALARS, pl.BlockSpec((count, width // NYH), lambda i: (0, i)), weight, weight],
        out_specs=pl.BlockSpec((count, head), lambda i: (0, 0)),
        out_shape=jax.ShapeDtypeStruct((count, head), bf16),
        scratch_shapes=[pltpu.VMEM((count, head), f32)],
        name="forward",
    )(core, tokens, mine, other)


def update_kernel(
    limit, place_ref, squares_ref, sums_ref, arrived_ref, master_ref, m_code_ref, v_code_ref,
    m_scale_ref, v_scale_ref, master_new_ref, m_code_new_ref, v_code_new_ref, m_scale_new_ref,
    v_scale_new_ref, secondary_ref,
):
    rows, head = master_ref.shape
    blocks = m_scale_ref.shape[0]
    height = rows // blocks
    total = jnp.sum(squares_ref[...], axis=0, keepdims=True)
    factor = limit / jnp.maximum(jnp.sqrt(total), limit)
    gradient = sums_ref[pl.ds(place_ref[0] * rows, rows), :]
    for b in range(blocks):
        at = slice(b * height, (b + 1) * height)
        scaled = factor * gradient[at]
        m_old = m_code_ref[...].astype(f32)[at] * m_scale_ref[b]
        v_old = v_code_ref[...].astype(f32)[at] * v_scale_ref[b]
        moment = 0.9 * m_old + 0.1 * scaled
        second = 0.95 * v_old + 0.05 * scaled * scaled
        old = master_ref[at, :]
        master_new_ref[at, :] = old - 0.01 * (moment / (jnp.sqrt(second) + 1e-08) + 0.1 * old)
        m_top = jnp.max(jnp.abs(moment)) + 1e-06
        v_top = jnp.max(second) + 1e-06
        m_scale_new_ref[b] = m_top
        v_scale_new_ref[b] = v_top
        m_code_new_ref[at, :] = (moment / m_top).astype(bf16)
        v_code_new_ref[at, :] = (second / v_top).astype(bf16)
    pad = jnp.zeros((SLOT - rows, head), f32)
    sums = sums_ref[...]
    new = []
    for zh in range(NZH):
        scaled = factor * jnp.concatenate([sums[zh * rows : (zh + 1) * rows], pad], axis=0)
        m_old, v_old, high, low = (
            arrived_ref[zh, NZH * rows + s * SLOT : NZH * rows + (s + 1) * SLOT, :].astype(f32)
            for s in range(4)
        )
        old = high + low
        moment = 0.9 * m_old + 0.1 * scaled
        second = 0.95 * v_old + 0.05 * scaled * scaled
        value = old - 0.01 * (moment / (jnp.sqrt(second) + 1e-08) + 0.1 * old)
        new.append(value[:rows])
    secondary_ref[...] = jnp.concatenate(new, axis=0).astype(bf16)


def update(limit, place, squares, sums, arrived, master, m_code, v_code, m_scale, v_scale):
    shape = jax.ShapeDtypeStruct
    return pl.pallas_call(
        functools.partial(update_kernel, limit),
        in_specs=[SCALARS] + [WHOLE] * 6 + [SCALARS] * 2,
        out_specs=[WHOLE] * 3 + [SCALARS] * 2 + [WHOLE],
        out_shape=[
            shape(master.shape, f32),
            shape(m_code.shape, bf16),
            shape(v_code.shape, bf16),
            shape(m_scale.shape, f32),
            shape(v_scale.shape, f32),
            shape(sums.shape, bf16),
        ],
        name="update",
    )(place, squares, sums, arrived, master, m_code, v_code, m_scale, v_scale)


def order_kernel(rows, pieces_ref, out_ref):
    near = pieces_ref.shape[0]
    pieces = [pieces_ref[k].astype(f32) for k in range(near)]
    for zh in range(NZH):
        at = slice(zh * near * rows, (zh + 1) * near * rows)
        block = jnp.concatenate([p[zh * rows : (zh + 1) * rows] for p in pieces], axis=0)
        out_ref[at, :] = block.astype(bf16)


def ordered(pieces, rows):
    near, height, head = pieces.shape
    return pl.pallas_call(
        functools.partial(order_kernel, rows),
        in_specs=[WHOLE],
        out_specs=WHOLE,
        out_shape=jax.ShapeDtypeStruct((near * height, head), bf16),
        name="ordered",
    )(pieces)


def body(tokens, cotangent, secondary, master, m_code, v_code, m_scale, v_scale):
    width, head = tokens.shape[1], cotangent.shape[1]
    rows, copy_rows = master.shape[0], secondary.shape[0]
    core = lax.axis_index("c")
    cores = core.reshape(1).astype(jnp.int32)
    weight = lax.dynamic_slice_in_dim(secondary, core * (copy_rows // 2), copy_rows // 2, 0)
    weight, tokens = lax.optimization_barrier((weight, tokens))
    mine = lax.all_gather(weight, INNER, axis=0, tiled=True)
    kept, sent, own_states = gradient_parts(
        cores, tokens, cotangent, master, m_code, v_code, m_scale, v_scale
    )
    kept = kept.reshape(NX * NYL, -1, head)
    other = swap_cores(sent.reshape(kept.shape))
    group = (kept.astype(f32) + other.astype(f32)).astype(bf16)
    group = exchange(group, ("x", "yl"))
    group = jnp.sum(group.astype(f32), axis=0).astype(bf16)
    group = exchange(group.reshape(NYH, -1, head), "yh")
    group = jnp.sum(group.astype(f32), axis=0).astype(bf16)
    group = exchange(group.reshape(NZL, NZH * rows, head), "zl")
    group = jnp.sum(group.astype(f32), axis=0).astype(bf16)
    arrived = to_all(jnp.concatenate([group, own_states], axis=0), "zh")
    sums = jnp.sum(arrived[:, : NZH * rows].astype(f32), axis=0)
    squares = jnp.sum(jnp.square(sums))
    squares = to_all(jnp.broadcast_to(squares, (1, head)), NEAR)
    squares, mine = lax.optimization_barrier((jnp.sum(squares, axis=0), mine))
    squares = to_all(squares, INNER)
    projected = forward(cores, tokens, mine, swap_cores(mine))
    squares, projected = lax.optimization_barrier((squares, projected))
    squares = squares.reshape(NYH * NX, head)
    limit = 0.25 * math.sqrt(width * head)
    place = lax.axis_index("zh").reshape(1).astype(jnp.int32)
    *results, piece = update(
        limit, place, squares, sums, arrived, master, m_code, v_code, m_scale, v_scale
    )
    return (projected, *results, ordered(to_all(piece, NEAR), rows))


def solution(mesh):
    split = Mesh(mesh.devices.reshape(4, 4, 2, 2, 4, 4), OUTER_INNER)
    return jax.shard_map(
        body,
        mesh=split,
        in_specs=(
            P(OUTER_INNER, None),
            P(OUTER_INNER, None),
            P(INNER, None),
            P(INNER_OUTER, None),
            P(INNER_OUTER, None),
            P(INNER_OUTER, None),
            P(INNER_OUTER),
            P(INNER_OUTER),
        ),
        out_specs=(
            P(OUTER_INNER, None),
            P(INNER_OUTER, None),
            P(INNER_OUTER, None),
            P(INNER_OUTER, None),
            P(INNER_OUTER),
            P(INNER_OUTER),
            P(INNER, None),
        ),
        check_vma=False,
    )
```

```python
import functools
import math

import jax
import jax.numpy as jnp
from jax import lax
from jax.experimental import pallas as pl
from jax.experimental.pallas import tpu as pltpu
from jax.sharding import Mesh
from jax.sharding import PartitionSpec as P

INNER = ("yh", "x")
OUTER = ("zh", "zl", "yl", "c")
OUTER_INNER = OUTER + INNER
INNER_OUTER = INNER + OUTER
NEAR = ("zl", "yl", "c")
NZH, NZL, NYL, NC, NYH, NX = 4, 4, 2, 2, 4, 4
STATES = 4
bf16, f32 = jnp.bfloat16, jnp.float32
WHOLE = pl.BlockSpec(memory_space=pltpu.VMEM)
SCALARS = pl.BlockSpec(memory_space=pltpu.SMEM)


def exchange(pieces, axes):
    return lax.all_to_all(pieces, axes, split_axis=0, concat_axis=0, tiled=True)


def to_all(value, axes):
    return exchange(jnp.broadcast_to(value, (lax.axis_size(axes), *value.shape)), axes)


def swap_cores(value):
    return lax.ppermute(value, "c", [(0, 1), (1, 0)])


def gradient_kernel(
    rows, core_ref, m_scale_ref, v_scale_ref, tokens_ref, cotangent_ref, secondary_ref, master_ref,
    m_code_ref, v_code_ref, kept_ref, sent_ref, weight_ref, states_ref,
):
    first = core_ref[0] == 0

    @pl.when(pl.program_id(0) == 0)
    def _():
        height = rows // m_scale_ref.shape[0]
        line = lax.broadcasted_iota(jnp.int32, master_ref.shape, 0)
        m_scale, v_scale = m_scale_ref[0], v_scale_ref[0]
        for b in range(1, m_scale_ref.shape[0]):
            m_scale = jnp.where(line < b * height, m_scale, m_scale_ref[b])
            v_scale = jnp.where(line < b * height, v_scale, v_scale_ref[b])
        master = master_ref[...]
        high = master.astype(bf16).astype(f32)
        states = (
            m_code_ref[...].astype(f32) * m_scale,
            v_code_ref[...].astype(f32) * v_scale,
            high,
            master - high,
        )
        states_ref[...] = jnp.concatenate(states, axis=0).astype(bf16)
        half = weight_ref.shape[0]
        weight_ref[...] = secondary_ref[pl.ds(pl.multiple_of(core_ref[0] * half, half), half), :]

    columns = tokens_ref.shape[1] // NX
    chip = NC * rows
    for x in range(NX):
        part = lax.dot_general(
            tokens_ref[:, x * columns : (x + 1) * columns],
            cotangent_ref[...],
            (((0,), (0,)), ((), ())),
            preferred_element_type=f32,
        )
        for yl in range(NYL):
            for zl in range(NZL):
                both = []
                for core in range(NC):
                    starts = [
                        ((NZL * zh + zl) * NYL + yl) * chip + core * rows for zh in range(NZH)
                    ]
                    both.append(jnp.concatenate([part[s : s + rows] for s in starts], axis=0))
                at = slice(zl * NZH * rows, (zl + 1) * NZH * rows)
                kept_ref[x, yl, 0, at, :] = jnp.where(first, both[0], both[1]).astype(bf16)
                sent_ref[x, yl, 0, at, :] = jnp.where(first, both[1], both[0]).astype(bf16)


def gradient_parts(core, tokens, cotangent, secondary, master, m_code, v_code, m_scale, v_scale):
    rows, copy_rows = master.shape[0], secondary.shape[0]
    states = (STATES * rows, master.shape[1])
    weight = (copy_rows // NC, master.shape[1])
    still = lambda i: (0, 0)
    count, width = tokens.shape
    head = cotangent.shape[1]
    span = NZH * NZL * rows
    shape = jax.ShapeDtypeStruct((NX, NYL, NYH, span, head), bf16)
    spec = pl.BlockSpec((NX, NYL, 1, span, head), lambda i: (0, 0, i, 0, 0))
    return pl.pallas_call(
        functools.partial(gradient_kernel, rows),
        grid=(NYH,),
        in_specs=[
            SCALARS,
            SCALARS,
            SCALARS,
            pl.BlockSpec((count, width // NYH), lambda i: (0, i)),
            pl.BlockSpec((count, head), still),
            pl.BlockSpec((copy_rows, head), still),
        ]
        + [pl.BlockSpec((rows, head), still)] * 3,
        out_specs=[spec, spec, pl.BlockSpec(weight, still), pl.BlockSpec(states, still)],
        out_shape=[
            shape,
            shape,
            jax.ShapeDtypeStruct(weight, bf16),
            jax.ShapeDtypeStruct(states, bf16),
        ],
        name="gradient_parts",
    )(core, m_scale, v_scale, tokens, cotangent, secondary, master, m_code, v_code)


def forward_kernel(core_ref, tokens_ref, mine_ref, other_ref, out_ref, total_ref):
    step = pl.program_id(0)
    core = core_ref[0]
    half = mine_ref.shape[0] // NX
    total = jnp.zeros(total_ref.shape, f32)
    for x in range(NX):
        own = pl.ds(pl.multiple_of((2 * x + core) * half, half), half)
        rest = pl.ds(pl.multiple_of((2 * x + 1 - core) * half, half), half)
        at = slice(x * half, (x + 1) * half)
        total += jnp.dot(tokens_ref[:, own], mine_ref[at, :], preferred_element_type=f32)
        total += jnp.dot(tokens_ref[:, rest], other_ref[at, :], preferred_element_type=f32)

    @pl.when(step == 0)
    def _():
        total_ref[...] = total

    @pl.when(step > 0)
    def _():
        total_ref[...] += total

    @pl.when(step == pl.num_programs(0) - 1)
    def _():
        out_ref[...] = total_ref[...].astype(bf16)


def forward(core, tokens, mine, other):
    count, width = tokens.shape
    height, head = mine.shape
    weight = pl.BlockSpec((height // NYH, head), lambda i: (i, 0))
    return pl.pallas_call(
        forward_kernel,
        grid=(NYH,),
        in_specs=[SCALARS, pl.BlockSpec((count, width // NYH), lambda i: (0, i)), weight, weight],
        out_specs=pl.BlockSpec((count, head), lambda i: (0, 0)),
        out_shape=jax.ShapeDtypeStruct((count, head), bf16),
        scratch_shapes=[pltpu.VMEM((count, head), f32)],
        name="forward",
    )(core, tokens, mine, other)


def update_kernel(
    limit, place_ref, squares_ref, sums_ref, arrived_ref, master_ref, m_code_ref, v_code_ref,
    m_scale_ref, v_scale_ref, master_new_ref, m_code_new_ref, v_code_new_ref, m_scale_new_ref,
    v_scale_new_ref, pieces_ref,
):
    rows, head = master_ref.shape
    blocks = m_scale_ref.shape[0]
    height = rows // blocks
    total = jnp.sum(squares_ref[...], axis=0, keepdims=True)
    factor = limit / jnp.maximum(jnp.sqrt(total), limit)
    gradient = sums_ref[pl.ds(place_ref[0] * rows, rows), :]
    for b in range(blocks):
        at = slice(b * height, (b + 1) * height)
        scaled = factor * gradient[at]
        m_old = m_code_ref[...].astype(f32)[at] * m_scale_ref[b]
        v_old = v_code_ref[...].astype(f32)[at] * v_scale_ref[b]
        moment = 0.9 * m_old + 0.1 * scaled
        second = 0.95 * v_old + 0.05 * scaled * scaled
        old = master_ref[at, :]
        master_new_ref[at, :] = old - 0.01 * (moment / (jnp.sqrt(second) + 1e-08) + 0.1 * old)
        m_top = jnp.max(jnp.abs(moment)) + 1e-06
        v_top = jnp.max(second) + 1e-06
        m_scale_new_ref[b] = m_top
        v_scale_new_ref[b] = v_top
        m_code_new_ref[at, :] = (moment / m_top).astype(bf16)
        v_code_new_ref[at, :] = (second / v_top).astype(bf16)
    sums = sums_ref[...]
    new = []
    for zh in range(NZH):
        scaled = factor * sums[zh * rows : (zh + 1) * rows]
        states = arrived_ref[zh, NZH * rows :, :].astype(f32)
        m_old, v_old, high, low = (states[s * rows : (s + 1) * rows] for s in range(STATES))
        old = high + low
        moment = 0.9 * m_old + 0.1 * scaled
        second = 0.95 * v_old + 0.05 * scaled * scaled
        new.append(old - 0.01 * (moment / (jnp.sqrt(second) + 1e-08) + 0.1 * old))
    piece = jnp.concatenate(new, axis=0).astype(bf16)
    for k in range(pieces_ref.shape[0]):
        pieces_ref[k] = piece


def update(limit, place, squares, sums, arrived, master, m_code, v_code, m_scale, v_scale):
    shape = jax.ShapeDtypeStruct
    return pl.pallas_call(
        functools.partial(update_kernel, limit),
        in_specs=[SCALARS] + [WHOLE] * 6 + [SCALARS] * 2,
        out_specs=[WHOLE] * 3 + [SCALARS] * 2 + [WHOLE],
        out_shape=[
            shape(master.shape, f32),
            shape(m_code.shape, bf16),
            shape(v_code.shape, bf16),
            shape(m_scale.shape, f32),
            shape(v_scale.shape, f32),
            shape((NZL * NYL * NC, *sums.shape), bf16),
        ],
        name="update",
    )(place, squares, sums, arrived, master, m_code, v_code, m_scale, v_scale)


def order_kernel(rows, pieces_ref, out_ref):
    near = pieces_ref.shape[0]
    pieces = [pieces_ref[k].astype(f32) for k in range(near)]
    for zh in range(NZH):
        at = slice(zh * near * rows, (zh + 1) * near * rows)
        block = jnp.concatenate([p[zh * rows : (zh + 1) * rows] for p in pieces], axis=0)
        out_ref[at, :] = block.astype(bf16)


def ordered(pieces, rows):
    near, height, head = pieces.shape
    return pl.pallas_call(
        functools.partial(order_kernel, rows),
        in_specs=[WHOLE],
        out_specs=WHOLE,
        out_shape=jax.ShapeDtypeStruct((near * height, head), bf16),
        name="ordered",
    )(pieces)


def body(tokens, cotangent, secondary, master, m_code, v_code, m_scale, v_scale):
    width, head = tokens.shape[1], cotangent.shape[1]
    rows = master.shape[0]
    core = lax.axis_index("c")
    cores = core.reshape(1).astype(jnp.int32)
    kept, sent, weight, own_states = gradient_parts(
        cores, tokens, cotangent, secondary, master, m_code, v_code, m_scale, v_scale
    )
    mine = lax.all_gather(weight, INNER, axis=0, tiled=True)
    kept = kept.reshape(NX * NYL, -1, head)
    other = swap_cores(sent.reshape(kept.shape))
    group = (kept.astype(f32) + other.astype(f32)).astype(bf16)
    group = exchange(group, ("x", "yl"))
    group = jnp.sum(group.astype(f32), axis=0).astype(bf16)
    group = exchange(group.reshape(NYH * NZL, NZH * rows, head), ("yh", "zl"))
    group = jnp.sum(group.astype(f32), axis=0).astype(bf16)
    arrived = to_all(jnp.concatenate([group, own_states], axis=0), "zh")
    sums = jnp.sum(arrived[:, : NZH * rows].astype(f32), axis=0)
    squares = jnp.sum(jnp.square(sums))
    squares = to_all(jnp.broadcast_to(squares, (1, head)), NEAR)
    squares, mine = lax.optimization_barrier((jnp.sum(squares, axis=0), mine))
    squares = to_all(squares, INNER)
    projected = forward(cores, tokens, mine, swap_cores(mine))
    squares, projected = lax.optimization_barrier((squares, projected))
    squares = squares.reshape(NYH * NX, head)
    limit = 0.25 * math.sqrt(width * head)
    place = lax.axis_index("zh").reshape(1).astype(jnp.int32)
    *results, pieces = update(
        limit, place, squares, sums, arrived, master, m_code, v_code, m_scale, v_scale
    )
    return (projected, *results, ordered(exchange(pieces, NEAR), rows))


def solution(mesh):
    split = Mesh(mesh.devices.reshape(4, 4, 2, 2, 4, 4), OUTER_INNER)
    return jax.shard_map(
        body,
        mesh=split,
        in_specs=(
            P(OUTER_INNER, None),
            P(OUTER_INNER, None),
            P(INNER, None),
            P(INNER_OUTER, None),
            P(INNER_OUTER, None),
            P(INNER_OUTER, None),
            P(INNER_OUTER),
            P(INNER_OUTER),
        ),
        out_specs=(
            P(OUTER_INNER, None),
            P(INNER_OUTER, None),
            P(INNER_OUTER, None),
            P(INNER_OUTER, None),
            P(INNER_OUTER),
            P(INNER_OUTER),
            P(INNER, None),
        ),
        check_vma=False,
    )
```

```python
import functools
import math

import jax
import jax.numpy as jnp
from jax import lax
from jax.experimental import pallas as pl
from jax.experimental.pallas import tpu as pltpu
from jax.sharding import Mesh
from jax.sharding import PartitionSpec as P

INNER = ("yh", "x")
OUTER = ("zh", "zm", "zp", "yl", "c")
OUTER_INNER = OUTER + INNER
INNER_OUTER = INNER + OUTER
NEAR = ("zm", "zp", "yl", "c")
NZH, NZM, NZP, NYL, NC, NYH, NX = 4, 2, 2, 2, 2, 4, 4
STATES = 4
bf16, f32 = jnp.bfloat16, jnp.float32
WHOLE = pl.BlockSpec(memory_space=pltpu.VMEM)
SCALARS = pl.BlockSpec(memory_space=pltpu.SMEM)


def exchange(pieces, axes):
    return lax.all_to_all(pieces, axes, split_axis=0, concat_axis=0, tiled=True)


def to_all(value, axes):
    return exchange(jnp.broadcast_to(value, (lax.axis_size(axes), *value.shape)), axes)


def swap_cores(value):
    return lax.ppermute(value, "c", [(0, 1), (1, 0)])


def gradient_kernel(
    rows, core_ref, m_scale_ref, v_scale_ref, tokens_ref, cotangent_ref, secondary_ref, master_ref,
    m_code_ref, v_code_ref, kept_ref, sent_ref, weight_ref, states_ref,
):
    first = core_ref[0] == 0

    @pl.when(pl.program_id(0) == 0)
    def _():
        height = rows // m_scale_ref.shape[0]
        line = lax.broadcasted_iota(jnp.int32, master_ref.shape, 0)
        m_scale, v_scale = m_scale_ref[0], v_scale_ref[0]
        for b in range(1, m_scale_ref.shape[0]):
            m_scale = jnp.where(line < b * height, m_scale, m_scale_ref[b])
            v_scale = jnp.where(line < b * height, v_scale, v_scale_ref[b])
        master = master_ref[...]
        high = master.astype(bf16).astype(f32)
        states = (
            m_code_ref[...].astype(f32) * m_scale,
            v_code_ref[...].astype(f32) * v_scale,
            high,
            master - high,
        )
        states_ref[...] = jnp.concatenate(states, axis=0).astype(bf16)
        half = weight_ref.shape[0]
        weight_ref[...] = secondary_ref[pl.ds(pl.multiple_of(core_ref[0] * half, half), half), :]

    columns = tokens_ref.shape[1] // NX
    chip = NC * rows
    for x in range(NX):
        part = lax.dot_general(
            tokens_ref[:, x * columns : (x + 1) * columns],
            cotangent_ref[...],
            (((0,), (0,)), ((), ())),
            preferred_element_type=f32,
        )
        for yl in range(NYL):
            for zp in range(NZP):
                for zm in range(NZM):
                    both = []
                    for core in range(NC):
                        starts = [
                            (((zh * NZM + zm) * NZP + zp) * NYL + yl) * chip + core * rows
                            for zh in range(NZH)
                        ]
                        both.append(jnp.concatenate([part[s : s + rows] for s in starts], axis=0))
                    at = slice(zm * NZH * rows, (zm + 1) * NZH * rows)
                    kept_ref[x, yl, zp, 0, at, :] = jnp.where(first, both[0], both[1]).astype(bf16)
                    sent_ref[x, yl, zp, 0, at, :] = jnp.where(first, both[1], both[0]).astype(bf16)


def gradient_parts(core, tokens, cotangent, secondary, master, m_code, v_code, m_scale, v_scale):
    rows, copy_rows = master.shape[0], secondary.shape[0]
    states = (STATES * rows, master.shape[1])
    weight = (copy_rows // NC, master.shape[1])
    still = lambda i: (0, 0)
    count, width = tokens.shape
    head = cotangent.shape[1]
    span = NZH * NZM * rows
    shape = jax.ShapeDtypeStruct((NX, NYL, NZP, NYH, span, head), bf16)
    spec = pl.BlockSpec((NX, NYL, NZP, 1, span, head), lambda i: (0, 0, 0, i, 0, 0))
    return pl.pallas_call(
        functools.partial(gradient_kernel, rows),
        grid=(NYH,),
        in_specs=[
            SCALARS,
            SCALARS,
            SCALARS,
            pl.BlockSpec((count, width // NYH), lambda i: (0, i)),
            pl.BlockSpec((count, head), still),
            pl.BlockSpec((copy_rows, head), still),
        ]
        + [pl.BlockSpec((rows, head), still)] * 3,
        out_specs=[spec, spec, pl.BlockSpec(weight, still), pl.BlockSpec(states, still)],
        out_shape=[
            shape,
            shape,
            jax.ShapeDtypeStruct(weight, bf16),
            jax.ShapeDtypeStruct(states, bf16),
        ],
        name="gradient_parts",
    )(core, m_scale, v_scale, tokens, cotangent, secondary, master, m_code, v_code)


def forward_kernel(core_ref, tokens_ref, mine_ref, other_ref, out_ref, total_ref):
    step = pl.program_id(0)
    core = core_ref[0]
    half = mine_ref.shape[0] // NX
    total = jnp.zeros(total_ref.shape, f32)
    for x in range(NX):
        own = pl.ds(pl.multiple_of((2 * x + core) * half, half), half)
        rest = pl.ds(pl.multiple_of((2 * x + 1 - core) * half, half), half)
        at = slice(x * half, (x + 1) * half)
        total += jnp.dot(tokens_ref[:, own], mine_ref[at, :], preferred_element_type=f32)
        total += jnp.dot(tokens_ref[:, rest], other_ref[at, :], preferred_element_type=f32)

    @pl.when(step == 0)
    def _():
        total_ref[...] = total

    @pl.when(step > 0)
    def _():
        total_ref[...] += total

    @pl.when(step == pl.num_programs(0) - 1)
    def _():
        out_ref[...] = total_ref[...].astype(bf16)


def forward(core, tokens, mine, other):
    count, width = tokens.shape
    height, head = mine.shape
    weight = pl.BlockSpec((height // NYH, head), lambda i: (i, 0))
    return pl.pallas_call(
        forward_kernel,
        grid=(NYH,),
        in_specs=[SCALARS, pl.BlockSpec((count, width // NYH), lambda i: (0, i)), weight, weight],
        out_specs=pl.BlockSpec((count, head), lambda i: (0, 0)),
        out_shape=jax.ShapeDtypeStruct((count, head), bf16),
        scratch_shapes=[pltpu.VMEM((count, head), f32)],
        name="forward",
    )(core, tokens, mine, other)


def update_kernel(
    limit, place_ref, squares_ref, sums_ref, arrived_ref, master_ref, m_code_ref, v_code_ref,
    m_scale_ref, v_scale_ref, master_new_ref, m_code_new_ref, v_code_new_ref, m_scale_new_ref,
    v_scale_new_ref, pieces_ref,
):
    rows, head = master_ref.shape
    blocks = m_scale_ref.shape[0]
    height = rows // blocks
    total = jnp.sum(squares_ref[...], axis=0, keepdims=True)
    factor = limit / jnp.maximum(jnp.sqrt(total), limit)
    gradient = sums_ref[pl.ds(place_ref[0] * rows, rows), :]
    for b in range(blocks):
        at = slice(b * height, (b + 1) * height)
        scaled = factor * gradient[at]
        m_old = m_code_ref[...].astype(f32)[at] * m_scale_ref[b]
        v_old = v_code_ref[...].astype(f32)[at] * v_scale_ref[b]
        moment = 0.9 * m_old + 0.1 * scaled
        second = 0.95 * v_old + 0.05 * scaled * scaled
        old = master_ref[at, :]
        master_new_ref[at, :] = old - 0.01 * (moment / (jnp.sqrt(second) + 1e-08) + 0.1 * old)
        m_top = jnp.max(jnp.abs(moment)) + 1e-06
        v_top = jnp.max(second) + 1e-06
        m_scale_new_ref[b] = m_top
        v_scale_new_ref[b] = v_top
        m_code_new_ref[at, :] = (moment / m_top).astype(bf16)
        v_code_new_ref[at, :] = (second / v_top).astype(bf16)
    sums = sums_ref[...]
    new = []
    for zh in range(NZH):
        scaled = factor * sums[zh * rows : (zh + 1) * rows]
        states = arrived_ref[zh, NZH * rows :, :].astype(f32)
        m_old, v_old, high, low = (states[s * rows : (s + 1) * rows] for s in range(STATES))
        old = high + low
        moment = 0.9 * m_old + 0.1 * scaled
        second = 0.95 * v_old + 0.05 * scaled * scaled
        new.append(old - 0.01 * (moment / (jnp.sqrt(second) + 1e-08) + 0.1 * old))
    piece = jnp.concatenate(new, axis=0).astype(bf16)
    for k in range(pieces_ref.shape[0]):
        pieces_ref[k] = piece


def update(limit, place, squares, sums, arrived, master, m_code, v_code, m_scale, v_scale):
    shape = jax.ShapeDtypeStruct
    return pl.pallas_call(
        functools.partial(update_kernel, limit),
        in_specs=[SCALARS] + [WHOLE] * 6 + [SCALARS] * 2,
        out_specs=[WHOLE] * 3 + [SCALARS] * 2 + [WHOLE],
        out_shape=[
            shape(master.shape, f32),
            shape(m_code.shape, bf16),
            shape(v_code.shape, bf16),
            shape(m_scale.shape, f32),
            shape(v_scale.shape, f32),
            shape((NZM * NZP * NYL * NC, *sums.shape), bf16),
        ],
        name="update",
    )(place, squares, sums, arrived, master, m_code, v_code, m_scale, v_scale)


def order_kernel(rows, pieces_ref, out_ref):
    near = pieces_ref.shape[0]
    pieces = [pieces_ref[k].astype(f32) for k in range(near)]
    for zh in range(NZH):
        at = slice(zh * near * rows, (zh + 1) * near * rows)
        block = jnp.concatenate([p[zh * rows : (zh + 1) * rows] for p in pieces], axis=0)
        out_ref[at, :] = block.astype(bf16)


def ordered(pieces, rows):
    near, height, head = pieces.shape
    return pl.pallas_call(
        functools.partial(order_kernel, rows),
        in_specs=[WHOLE],
        out_specs=WHOLE,
        out_shape=jax.ShapeDtypeStruct((near * height, head), bf16),
        name="ordered",
    )(pieces)


def body(tokens, cotangent, secondary, master, m_code, v_code, m_scale, v_scale):
    width, head = tokens.shape[1], cotangent.shape[1]
    rows = master.shape[0]
    core = lax.axis_index("c")
    cores = core.reshape(1).astype(jnp.int32)
    kept, sent, weight, own_states = gradient_parts(
        cores, tokens, cotangent, secondary, master, m_code, v_code, m_scale, v_scale
    )
    mine = lax.all_gather(weight, INNER, axis=0, tiled=True)
    kept = kept.reshape(NX * NYL * NZP, -1, head)
    other = swap_cores(sent.reshape(kept.shape))
    group = (kept.astype(f32) + other.astype(f32)).astype(bf16)
    group = exchange(group, ("x", "yl", "zp"))
    group = jnp.sum(group.astype(f32), axis=0).astype(bf16)
    group = exchange(group.reshape(NYH * NZM, NZH * rows, head), ("yh", "zm"))
    group = jnp.sum(group.astype(f32), axis=0).astype(bf16)
    arrived = to_all(jnp.concatenate([group, own_states], axis=0), "zh")
    sums = jnp.sum(arrived[:, : NZH * rows].astype(f32), axis=0)
    squares = jnp.sum(jnp.square(sums))
    squares = to_all(jnp.broadcast_to(squares, (1, head)), NEAR)
    squares, mine = lax.optimization_barrier((jnp.sum(squares, axis=0), mine))
    squares = to_all(squares, INNER)
    other = swap_cores(mine)
    squares = squares.reshape(NYH * NX, head)
    limit = 0.25 * math.sqrt(width * head)
    place = lax.axis_index("zh").reshape(1).astype(jnp.int32)
    *results, pieces = update(
        limit, place, squares, sums, arrived, master, m_code, v_code, m_scale, v_scale
    )
    pieces = exchange(pieces, NEAR)
    projected = forward(cores, tokens, mine, other)
    pieces, projected = lax.optimization_barrier((pieces, projected))
    return (projected, *results, ordered(pieces, rows))


def solution(mesh):
    split = Mesh(mesh.devices.reshape(4, 2, 2, 2, 2, 4, 4), OUTER_INNER)
    return jax.shard_map(
        body,
        mesh=split,
        in_specs=(
            P(OUTER_INNER, None),
            P(OUTER_INNER, None),
            P(INNER, None),
            P(INNER_OUTER, None),
            P(INNER_OUTER, None),
            P(INNER_OUTER, None),
            P(INNER_OUTER),
            P(INNER_OUTER),
        ),
        out_specs=(
            P(OUTER_INNER, None),
            P(INNER_OUTER, None),
            P(INNER_OUTER, None),
            P(INNER_OUTER, None),
            P(INNER_OUTER),
            P(INNER_OUTER),
            P(INNER, None),
        ),
        check_vma=False,
    )
```

```python
import functools
import math

import jax
import jax.numpy as jnp
from jax import lax
from jax.experimental import pallas as pl
from jax.experimental.pallas import tpu as pltpu
from jax.sharding import Mesh
from jax.sharding import PartitionSpec as P


INNER = ("yh", "x")
OUTER = ("zh", "zm", "zp", "yl", "c")
OUTER_INNER = OUTER + INNER
INNER_OUTER = INNER + OUTER
NEAR = ("zm", "zp", "yl", "c")
NZH, NZM, NZP, NYL, NC, NYH, NX = 4, 2, 2, 2, 2, 4, 4
STATES = 4
bf16, f32 = jnp.bfloat16, jnp.float32
WHOLE = pl.BlockSpec(memory_space=pltpu.VMEM)
SCALARS = pl.BlockSpec(memory_space=pltpu.SMEM)


def exchange(pieces, axes):
    return lax.all_to_all(pieces, axes, split_axis=0, concat_axis=0, tiled=True)


def column_sums(value, copies):
    ones = jnp.ones((copies, value.shape[0]), f32)
    return jnp.dot(ones, value, precision=lax.Precision.HIGHEST)


def swap_cores(value):
    return lax.ppermute(value, "c", [(0, 1), (1, 0)])


def gradient_kernel(
    rows, core_ref, m_scale_ref, v_scale_ref, tokens_ref, cotangent_ref, secondary_ref, master_ref,
    m_code_ref, v_code_ref, kept_ref, sent_ref, weight_ref, states_ref,
):
    first = core_ref[0] == 0

    @pl.when(pl.program_id(0) == 0)
    def _():
        height = rows // m_scale_ref.shape[0]
        line = lax.broadcasted_iota(jnp.int32, master_ref.shape, 0)
        m_scale, v_scale = m_scale_ref[0], v_scale_ref[0]
        for b in range(1, m_scale_ref.shape[0]):
            m_scale = jnp.where(line < b * height, m_scale, m_scale_ref[b])
            v_scale = jnp.where(line < b * height, v_scale, v_scale_ref[b])
        master = master_ref[...]
        high = master.astype(bf16).astype(f32)
        states = (
            m_code_ref[...].astype(f32) * m_scale,
            v_code_ref[...].astype(f32) * v_scale,
            high,
            master - high,
        )
        states = jnp.concatenate(states, axis=0).astype(bf16)
        for zh in range(NZH):
            states_ref[zh, : NZH * rows, :] = jnp.zeros((NZH * rows, states.shape[1]), bf16)
            states_ref[zh, NZH * rows :, :] = states
        half = weight_ref.shape[0]
        weight_ref[...] = secondary_ref[pl.ds(pl.multiple_of(core_ref[0] * half, half), half), :]

    columns = tokens_ref.shape[1] // NX
    chip = NC * rows
    for x in range(NX):
        part = lax.dot_general(
            tokens_ref[:, x * columns : (x + 1) * columns],
            cotangent_ref[...],
            (((0,), (0,)), ((), ())),
            preferred_element_type=f32,
        )
        for yl in range(NYL):
            for zp in range(NZP):
                for zm in range(NZM):
                    both = []
                    for core in range(NC):
                        starts = [
                            (((zh * NZM + zm) * NZP + zp) * NYL + yl) * chip + core * rows
                            for zh in range(NZH)
                        ]
                        both.append(jnp.concatenate([part[s : s + rows] for s in starts], axis=0))
                    at = slice(zm * NZH * rows, (zm + 1) * NZH * rows)
                    kept_ref[x, yl, zp, 0, at, :] = jnp.where(first, both[0], both[1]).astype(bf16)
                    sent_ref[x, yl, zp, 0, at, :] = jnp.where(first, both[1], both[0]).astype(bf16)


def gradient_parts(core, tokens, cotangent, secondary, master, m_code, v_code, m_scale, v_scale):
    rows, copy_rows = master.shape[0], secondary.shape[0]
    states = (NZH, (NZH + STATES) * rows, master.shape[1])
    weight = (copy_rows // NC, master.shape[1])
    still = lambda i: (0, 0)
    count, width = tokens.shape
    head = cotangent.shape[1]
    span = NZH * NZM * rows
    shape = jax.ShapeDtypeStruct((NX, NYL, NZP, NYH, span, head), bf16)
    spec = pl.BlockSpec((NX, NYL, NZP, 1, span, head), lambda i: (0, 0, 0, i, 0, 0))
    return pl.pallas_call(
        functools.partial(gradient_kernel, rows),
        grid=(NYH,),
        in_specs=[
            SCALARS,
            SCALARS,
            SCALARS,
            pl.BlockSpec((count, width // NYH), lambda i: (0, i)),
            pl.BlockSpec((count, head), still),
            pl.BlockSpec((copy_rows, head), still),
        ]
        + [pl.BlockSpec((rows, head), still)] * 3,
        out_specs=[spec, spec, pl.BlockSpec(weight, still), pl.BlockSpec(states, lambda i: (0, 0, 0))],
        out_shape=[
            shape,
            shape,
            jax.ShapeDtypeStruct(weight, bf16),
            jax.ShapeDtypeStruct(states, bf16),
        ],
        name="gradient_parts",
    )(core, m_scale, v_scale, tokens, cotangent, secondary, master, m_code, v_code)


def forward_kernel(core_ref, tokens_ref, mine_ref, other_ref, out_ref, total_ref):
    step = pl.program_id(0)
    core = core_ref[0]
    half = mine_ref.shape[0] // NX
    total = jnp.zeros(total_ref.shape, f32)
    for x in range(NX):
        own = pl.ds(pl.multiple_of((2 * x + core) * half, half), half)
        rest = pl.ds(pl.multiple_of((2 * x + 1 - core) * half, half), half)
        at = slice(x * half, (x + 1) * half)
        total += jnp.dot(tokens_ref[:, own], mine_ref[at, :], preferred_element_type=f32)
        total += jnp.dot(tokens_ref[:, rest], other_ref[at, :], preferred_element_type=f32)

    @pl.when(step == 0)
    def _():
        total_ref[...] = total

    @pl.when(step > 0)
    def _():
        total_ref[...] += total

    @pl.when(step == pl.num_programs(0) - 1)
    def _():
        out_ref[...] = total_ref[...].astype(bf16)


def forward(core, tokens, mine, other):
    count, width = tokens.shape
    height, head = mine.shape
    weight = pl.BlockSpec((height // NYH, head), lambda i: (i, 0))
    return pl.pallas_call(
        forward_kernel,
        grid=(NYH,),
        in_specs=[SCALARS, pl.BlockSpec((count, width // NYH), lambda i: (0, i)), weight, weight],
        out_specs=pl.BlockSpec((count, head), lambda i: (0, 0)),
        out_shape=jax.ShapeDtypeStruct((count, head), bf16),
        scratch_shapes=[pltpu.VMEM((count, head), f32)],
        name="forward",
    )(core, tokens, mine, other)


def update_kernel(
    limit, place_ref, squares_ref, sums_ref, arrived_ref, master_ref, m_code_ref, v_code_ref,
    m_scale_ref, v_scale_ref, master_new_ref, m_code_new_ref, v_code_new_ref, m_scale_new_ref,
    v_scale_new_ref, pieces_ref,
):
    rows, _ = master_ref.shape
    blocks = m_scale_ref.shape[0]
    height = rows // blocks
    total = jnp.sum(squares_ref[...], axis=(0, 1), keepdims=True)
    factor = limit / jnp.maximum(jnp.sqrt(total), limit)
    gradient = sums_ref[pl.ds(place_ref[0] * rows, rows), :]
    for b in range(blocks):
        at = slice(b * height, (b + 1) * height)
        scaled = factor * gradient[at]
        m_old = m_code_ref[...].astype(f32)[at] * m_scale_ref[b]
        v_old = v_code_ref[...].astype(f32)[at] * v_scale_ref[b]
        moment = 0.9 * m_old + 0.1 * scaled
        second = 0.95 * v_old + 0.05 * scaled * scaled
        old = master_ref[at, :]
        master_new_ref[at, :] = old - 0.01 * (moment / (jnp.sqrt(second) + 1e-08) + 0.1 * old)
        m_top = jnp.max(jnp.abs(moment)) + 1e-06
        v_top = jnp.max(second) + 1e-06
        m_scale_new_ref[b] = m_top
        v_scale_new_ref[b] = v_top
        m_code_new_ref[at, :] = (moment / m_top).astype(bf16)
        v_code_new_ref[at, :] = (second / v_top).astype(bf16)
    sums = sums_ref[...]
    new = []
    for zh in range(NZH):
        scaled = factor * sums[zh * rows : (zh + 1) * rows]
        states = arrived_ref[zh, NZH * rows :, :].astype(f32)
        m_old, v_old, high, low = (states[s * rows : (s + 1) * rows] for s in range(STATES))
        old = high + low
        moment = 0.9 * m_old + 0.1 * scaled
        second = 0.95 * v_old + 0.05 * scaled * scaled
        new.append(old - 0.01 * (moment / (jnp.sqrt(second) + 1e-08) + 0.1 * old))
    piece = jnp.concatenate(new, axis=0).astype(bf16)
    for k in range(pieces_ref.shape[0]):
        pieces_ref[k] = piece


def update(limit, place, squares, sums, arrived, master, m_code, v_code, m_scale, v_scale):
    shape = jax.ShapeDtypeStruct
    return pl.pallas_call(
        functools.partial(update_kernel, limit),
        in_specs=[SCALARS] + [WHOLE] * 6 + [SCALARS] * 2,
        out_specs=[WHOLE] * 3 + [SCALARS] * 2 + [WHOLE],
        out_shape=[
            shape(master.shape, f32),
            shape(m_code.shape, bf16),
            shape(v_code.shape, bf16),
            shape(m_scale.shape, f32),
            shape(v_scale.shape, f32),
            shape((NZM * NZP * NYL * NC, *sums.shape), bf16),
        ],
        name="update",
    )(place, squares, sums, arrived, master, m_code, v_code, m_scale, v_scale)


def order_kernel(rows, pieces_ref, out_ref):
    near = pieces_ref.shape[0]
    pieces = [pieces_ref[k].astype(f32) for k in range(near)]
    for zh in range(NZH):
        at = slice(zh * near * rows, (zh + 1) * near * rows)
        block = jnp.concatenate([p[zh * rows : (zh + 1) * rows] for p in pieces], axis=0)
        out_ref[at, :] = block.astype(bf16)


def ordered(pieces, rows):
    near, height, head = pieces.shape
    return pl.pallas_call(
        functools.partial(order_kernel, rows),
        in_specs=[WHOLE],
        out_specs=WHOLE,
        out_shape=jax.ShapeDtypeStruct((near * height, head), bf16),
        name="ordered",
    )(pieces)


def body(tokens, cotangent, secondary, master, m_code, v_code, m_scale, v_scale):
    width, head = tokens.shape[1], cotangent.shape[1]
    rows = master.shape[0]
    core = lax.axis_index("c")
    cores = core.reshape(1).astype(jnp.int32)
    kept, sent, weight, own_states = gradient_parts(
        cores, tokens, cotangent, secondary, master, m_code, v_code, m_scale, v_scale
    )
    mine = lax.all_gather(weight, INNER, axis=0, tiled=True)
    kept = kept.reshape(NX * NYL * NZP, -1, head)
    other = swap_cores(sent.reshape(kept.shape))
    group = (kept.astype(f32) + other.astype(f32)).astype(bf16)
    group = exchange(group, ("x", "yl", "zp"))
    group = jnp.sum(group.astype(f32), axis=0).astype(bf16)
    group = exchange(group.reshape(NYH * NZM, NZH * rows, head), ("yh", "zm"))
    group = jnp.sum(group.astype(f32), axis=0).astype(bf16)
    group = jnp.broadcast_to(group, (NZH, *group.shape))
    arrived = exchange(lax.dynamic_update_slice(own_states, group, (0, 0, 0)), "zh")
    sums = jnp.sum(arrived[:, : NZH * rows].astype(f32), axis=0)
    squares = column_sums(jnp.square(sums), lax.axis_size(NEAR))
    squares = column_sums(exchange(squares, NEAR), lax.axis_size(INNER))
    squares, mine = lax.optimization_barrier((squares, mine))
    squares = exchange(squares, INNER)
    other = swap_cores(mine)
    limit = 0.25 * math.sqrt(width * head)
    place = lax.axis_index("zh").reshape(1).astype(jnp.int32)
    *results, pieces = update(
        limit, place, squares, sums, arrived, master, m_code, v_code, m_scale, v_scale
    )
    pieces = exchange(pieces, NEAR)
    projected = forward(cores, tokens, mine, other)
    pieces, projected = lax.optimization_barrier((pieces, projected))
    return (projected, *results, ordered(pieces, rows))


def solution(mesh):
    split = Mesh(mesh.devices.reshape(4, 2, 2, 2, 2, 4, 4), OUTER_INNER)
    return jax.shard_map(
        body,
        mesh=split,
        in_specs=(
            P(OUTER_INNER, None),
            P(OUTER_INNER, None),
            P(INNER, None),
            P(INNER_OUTER, None),
            P(INNER_OUTER, None),
            P(INNER_OUTER, None),
            P(INNER_OUTER),
            P(INNER_OUTER),
        ),
        out_specs=(
            P(OUTER_INNER, None),
            P(INNER_OUTER, None),
            P(INNER_OUTER, None),
            P(INNER_OUTER, None),
            P(INNER_OUTER),
            P(INNER_OUTER),
            P(INNER, None),
        ),
        check_vma=False,
    )
```

```python
import functools
import itertools
import math

import jax
import jax.numpy as jnp
from jax import lax
from jax.experimental import pallas as pl
from jax.experimental.pallas import tpu as pltpu
from jax.sharding import Mesh
from jax.sharding import PartitionSpec as P


INNER = ("yh", "x")
OUTER = ("zh", "zm", "zp", "yl", "c")
OUTER_INNER = OUTER + INNER
INNER_OUTER = INNER + OUTER
NEAR = ("zm", "zp", "yl", "c")
NZH, NZM, NZP, NYL, NC, NYH, NX = 4, 2, 2, 2, 2, 4, 4
STATES = 4
STEPS = 2
bf16, f32 = jnp.bfloat16, jnp.float32
WHOLE = pl.BlockSpec(memory_space=pltpu.VMEM)
SCALARS = pl.BlockSpec(memory_space=pltpu.SMEM)


def exchange(pieces, axes):
    return lax.all_to_all(pieces, axes, split_axis=0, concat_axis=0, tiled=True)


def column_sums(value, copies):
    ones = jnp.ones((copies, value.shape[0]), f32)
    return jnp.dot(ones, value, precision=lax.Precision.HIGHEST)


def swap_cores(value):
    return lax.ppermute(value, "c", [(0, 1), (1, 0)])


def gradient_kernel(
    rows, core_ref, m_scale_ref, v_scale_ref, tokens_ref, cotangent_ref, secondary_ref, master_ref,
    m_code_ref, v_code_ref, kept_ref, sent_ref, weight_ref, states_ref,
):
    first = core_ref[0] == 0

    @pl.when(pl.program_id(0) == 0)
    def _():
        height = rows // m_scale_ref.shape[0]
        line = lax.broadcasted_iota(jnp.int32, master_ref.shape, 0)
        m_scale, v_scale = m_scale_ref[0], v_scale_ref[0]
        for b in range(1, m_scale_ref.shape[0]):
            m_scale = jnp.where(line < b * height, m_scale, m_scale_ref[b])
            v_scale = jnp.where(line < b * height, v_scale, v_scale_ref[b])
        master = master_ref[...]
        high = master.astype(bf16).astype(f32)
        states = (
            m_code_ref[...].astype(f32) * m_scale,
            v_code_ref[...].astype(f32) * v_scale,
            high,
            master - high,
        )
        states = jnp.concatenate(states, axis=0).astype(bf16)
        for zh in range(NZH):
            states_ref[zh, : NZH * rows, :] = jnp.zeros((NZH * rows, states.shape[1]), bf16)
            states_ref[zh, NZH * rows :, :] = states
        half = weight_ref.shape[0]
        weight_ref[...] = secondary_ref[pl.ds(pl.multiple_of(core_ref[0] * half, half), half), :]

    deep = kept_ref.shape[3]
    columns = tokens_ref.shape[1] // (deep * NX)
    chip = NC * rows
    for y, x in itertools.product(range(deep), range(NX)):
        start = (y * NX + x) * columns
        part = lax.dot_general(
            tokens_ref[:, start : start + columns],
            cotangent_ref[...],
            (((0,), (0,)), ((), ())),
            preferred_element_type=f32,
        )
        for yl in range(NYL):
            for zp in range(NZP):
                for zm in range(NZM):
                    both = []
                    for core in range(NC):
                        starts = [
                            (((zh * NZM + zm) * NZP + zp) * NYL + yl) * chip + core * rows
                            for zh in range(NZH)
                        ]
                        both.append(jnp.concatenate([part[s : s + rows] for s in starts], axis=0))
                    at = slice(zm * NZH * rows, (zm + 1) * NZH * rows)
                    kept_ref[x, yl, zp, y, at, :] = jnp.where(first, both[0], both[1]).astype(bf16)
                    sent_ref[x, yl, zp, y, at, :] = jnp.where(first, both[1], both[0]).astype(bf16)


def gradient_parts(core, tokens, cotangent, secondary, master, m_code, v_code, m_scale, v_scale):
    rows, copy_rows = master.shape[0], secondary.shape[0]
    states = (NZH, (NZH + STATES) * rows, master.shape[1])
    weight = (copy_rows // NC, master.shape[1])
    still = lambda i: (0, 0)
    count, width = tokens.shape
    head = cotangent.shape[1]
    span = NZH * NZM * rows
    shape = jax.ShapeDtypeStruct((NX, NYL, NZP, NYH, span, head), bf16)
    spec = pl.BlockSpec((NX, NYL, NZP, NYH // STEPS, span, head), lambda i: (0, 0, 0, i, 0, 0))
    return pl.pallas_call(
        functools.partial(gradient_kernel, rows),
        grid=(STEPS,),
        in_specs=[
            SCALARS,
            SCALARS,
            SCALARS,
            pl.BlockSpec((count, width // STEPS), lambda i: (0, i)),
            pl.BlockSpec((count, head), still),
            pl.BlockSpec((copy_rows, head), still),
        ]
        + [pl.BlockSpec((rows, head), still)] * 3,
        out_specs=[spec, spec, pl.BlockSpec(weight, still), pl.BlockSpec(states, lambda i: (0, 0, 0))],
        out_shape=[
            shape,
            shape,
            jax.ShapeDtypeStruct(weight, bf16),
            jax.ShapeDtypeStruct(states, bf16),
        ],
        name="gradient_parts",
    )(core, m_scale, v_scale, tokens, cotangent, secondary, master, m_code, v_code)


def forward_kernel(core_ref, tokens_ref, mine_ref, other_ref, out_ref, total_ref):
    step = pl.program_id(0)
    core = core_ref[0]
    shards = NYH * NX // STEPS
    half = mine_ref.shape[0] // shards
    total = jnp.zeros(total_ref.shape, f32)
    for x in range(shards):
        own = pl.ds(pl.multiple_of((2 * x + core) * half, half), half)
        rest = pl.ds(pl.multiple_of((2 * x + 1 - core) * half, half), half)
        at = slice(x * half, (x + 1) * half)
        total += jnp.dot(tokens_ref[:, own], mine_ref[at, :], preferred_element_type=f32)
        total += jnp.dot(tokens_ref[:, rest], other_ref[at, :], preferred_element_type=f32)

    @pl.when(step == 0)
    def _():
        total_ref[...] = total

    @pl.when(step > 0)
    def _():
        total_ref[...] += total

    @pl.when(step == pl.num_programs(0) - 1)
    def _():
        out_ref[...] = total_ref[...].astype(bf16)


def forward(core, tokens, mine, other):
    count, width = tokens.shape
    height, head = mine.shape
    weight = pl.BlockSpec((height // STEPS, head), lambda i: (i, 0))
    return pl.pallas_call(
        forward_kernel,
        grid=(STEPS,),
        in_specs=[SCALARS, pl.BlockSpec((count, width // STEPS), lambda i: (0, i)), weight, weight],
        out_specs=pl.BlockSpec((count, head), lambda i: (0, 0)),
        out_shape=jax.ShapeDtypeStruct((count, head), bf16),
        scratch_shapes=[pltpu.VMEM((count, head), f32)],
        name="forward",
    )(core, tokens, mine, other)


def clip_factor(limit, squares_ref):
    total = jnp.sum(squares_ref[...], axis=(0, 1), keepdims=True)
    return limit / jnp.maximum(jnp.sqrt(total), limit)


def own_kernel(
    limit, place_ref, squares_ref, sums_ref, master_ref, m_code_ref, v_code_ref, m_scale_ref,
    v_scale_ref, master_new_ref, m_code_new_ref, v_code_new_ref, m_scale_new_ref, v_scale_new_ref,
):
    rows = master_ref.shape[0]
    blocks = m_scale_ref.shape[0]
    height = rows // blocks
    factor = clip_factor(limit, squares_ref)
    gradient = sums_ref[pl.ds(place_ref[0] * rows, rows), :]
    for b in range(blocks):
        at = slice(b * height, (b + 1) * height)
        scaled = factor * gradient[at]
        m_old = m_code_ref[...].astype(f32)[at] * m_scale_ref[b]
        v_old = v_code_ref[...].astype(f32)[at] * v_scale_ref[b]
        moment = 0.9 * m_old + 0.1 * scaled
        second = 0.95 * v_old + 0.05 * scaled * scaled
        old = master_ref[at, :]
        master_new_ref[at, :] = old - 0.01 * (moment / (jnp.sqrt(second) + 1e-08) + 0.1 * old)
        m_top = jnp.max(jnp.abs(moment)) + 1e-06
        v_top = jnp.max(second) + 1e-06
        m_scale_new_ref[b] = m_top
        v_scale_new_ref[b] = v_top
        m_code_new_ref[at, :] = (moment / m_top).astype(bf16)
        v_code_new_ref[at, :] = (second / v_top).astype(bf16)


def own_update(limit, place, squares, sums, master, m_code, v_code, m_scale, v_scale):
    shape = jax.ShapeDtypeStruct
    return pl.pallas_call(
        functools.partial(own_kernel, limit),
        in_specs=[SCALARS] + [WHOLE] * 5 + [SCALARS] * 2,
        out_specs=[WHOLE] * 3 + [SCALARS] * 2,
        out_shape=[
            shape(master.shape, f32),
            shape(m_code.shape, bf16),
            shape(v_code.shape, bf16),
            shape(m_scale.shape, f32),
            shape(v_scale.shape, f32),
        ],
        name="own_update",
    )(place, squares, sums, master, m_code, v_code, m_scale, v_scale)


def copy_kernel(limit, rows, squares_ref, sums_ref, arrived_ref, pieces_ref):
    factor = clip_factor(limit, squares_ref)
    sums = sums_ref[...]
    new = []
    for zh in range(NZH):
        scaled = factor * sums[zh * rows : (zh + 1) * rows]
        states = arrived_ref[zh, NZH * rows :, :].astype(f32)
        m_old, v_old, high, low = (states[s * rows : (s + 1) * rows] for s in range(STATES))
        old = high + low
        moment = 0.9 * m_old + 0.1 * scaled
        second = 0.95 * v_old + 0.05 * scaled * scaled
        new.append(old - 0.01 * (moment / (jnp.sqrt(second) + 1e-08) + 0.1 * old))
    piece = jnp.concatenate(new, axis=0).astype(bf16)
    for k in range(pieces_ref.shape[0]):
        pieces_ref[k] = piece


def copy_update(limit, rows, squares, sums, arrived):
    return pl.pallas_call(
        functools.partial(copy_kernel, limit, rows),
        in_specs=[WHOLE] * 3,
        out_specs=WHOLE,
        out_shape=jax.ShapeDtypeStruct((NZM * NZP * NYL * NC, *sums.shape), bf16),
        name="copy_update",
    )(squares, sums, arrived)


def order_kernel(rows, pieces_ref, out_ref):
    near = pieces_ref.shape[0]
    pieces = [pieces_ref[k].astype(f32) for k in range(near)]
    for zh in range(NZH):
        at = slice(zh * near * rows, (zh + 1) * near * rows)
        block = jnp.concatenate([p[zh * rows : (zh + 1) * rows] for p in pieces], axis=0)
        out_ref[at, :] = block.astype(bf16)


def ordered(pieces, rows):
    near, height, head = pieces.shape
    return pl.pallas_call(
        functools.partial(order_kernel, rows),
        in_specs=[WHOLE],
        out_specs=WHOLE,
        out_shape=jax.ShapeDtypeStruct((near * height, head), bf16),
        name="ordered",
    )(pieces)


def body(tokens, cotangent, secondary, master, m_code, v_code, m_scale, v_scale):
    width, head = tokens.shape[1], cotangent.shape[1]
    rows = master.shape[0]
    core = lax.axis_index("c")
    cores = core.reshape(1).astype(jnp.int32)
    kept, sent, weight, own_states = gradient_parts(
        cores, tokens, cotangent, secondary, master, m_code, v_code, m_scale, v_scale
    )
    mine = lax.all_gather(weight, INNER, axis=0, tiled=True)
    kept = kept.reshape(NX * NYL * NZP, -1, head)
    other = swap_cores(sent.reshape(kept.shape))
    group = (kept.astype(f32) + other.astype(f32)).astype(bf16)
    group = exchange(group, ("x", "yl", "zp"))
    group = jnp.sum(group.astype(f32), axis=0).astype(bf16)
    group = exchange(group.reshape(NYH * NZM, NZH * rows, head), ("yh", "zm"))
    group = jnp.sum(group.astype(f32), axis=0).astype(bf16)
    group = jnp.broadcast_to(group, (NZH, *group.shape))
    arrived = exchange(lax.dynamic_update_slice(own_states, group, (0, 0, 0)), "zh")
    sums = jnp.sum(arrived[:, : NZH * rows].astype(f32), axis=0)
    squares = column_sums(jnp.square(sums), lax.axis_size(NEAR))
    squares = column_sums(exchange(squares, NEAR), lax.axis_size(INNER))
    squares, mine = lax.optimization_barrier((squares, mine))
    squares = exchange(squares, INNER)
    other = swap_cores(mine)
    limit = 0.25 * math.sqrt(width * head)
    place = lax.axis_index("zh").reshape(1).astype(jnp.int32)
    pieces = exchange(copy_update(limit, rows, squares, sums, arrived), NEAR)
    other, sums = lax.optimization_barrier((other, sums))
    results = own_update(
        limit, place, squares, sums, master, m_code, v_code, m_scale, v_scale
    )
    results, mine = lax.optimization_barrier((results, mine))
    projected = forward(cores, tokens, mine, other)
    pieces, projected, results = lax.optimization_barrier((pieces, projected, results))
    return (projected, *results, ordered(pieces, rows))


def solution(mesh):
    split = Mesh(mesh.devices.reshape(4, 2, 2, 2, 2, 4, 4), OUTER_INNER)
    return jax.shard_map(
        body,
        mesh=split,
        in_specs=(
            P(OUTER_INNER, None),
            P(OUTER_INNER, None),
            P(INNER, None),
            P(INNER_OUTER, None),
            P(INNER_OUTER, None),
            P(INNER_OUTER, None),
            P(INNER_OUTER),
            P(INNER_OUTER),
        ),
        out_specs=(
            P(OUTER_INNER, None),
            P(INNER_OUTER, None),
            P(INNER_OUTER, None),
            P(INNER_OUTER, None),
            P(INNER_OUTER),
            P(INNER_OUTER),
            P(INNER, None),
        ),
        check_vma=False,
    )
```
